32 devices in a mesh: gx: 4 (over z), gy: 8 (over y, x, core).
Axes of the slice: x: 2, y: 2, z: 4, core: 2. Of those that a mesh axis runs over, the one named last changes fastest.
Arguments:
- heat_source: float32 [1536, 1024], P(('gx', 'gy')), may hold values from -18 to 18
- stiffness: float32 [512, 384, 384], P(('gx', 'gy')), may hold values from -1 to 32, as said below
- element_faces: int32 [512, 6], P(('gx', 'gy')), may hold values from 0 to 1535, as said below
Outputs:
- solution: float32 [1536, 1024], P(('gx', 'gy'))
- residual: float32 [1536, 1024], P(('gx', 'gy'))
The draws below stay inside these ranges and needn't reach their ends.
Inputs may be any that keep to these rules, and one draw needn't show every extreme that they name: `element_faces`: the elements form a periodic grid of 8 x 16 x 4 hexahedra; device (i, j) of gx and gy holds the block of 2 x 2 x 4 elements at streamwise block i and spanwise block j, in a local order of its own, and owns the lower x, lower y and lower z faces of its elements, numbered in an order of its own. So every face number appears exactly twice, and a device's elements reference faces of itself, of the next device along gx (cyclic, same gy index; exactly 8 references) and of the next device along gy (cyclic, same gx index; exactly 8 references). `stiffness`: each element matrix is symmetric with a positive diagonal and strictly diagonally dominant.
All inputs are finite; a program needn't handle non-finite values.
Results may differ from the reference program's by a relative error of at most 0.0002.
Values sent between devices are 32-bit elements; how exact they have to be, the bound alone decides.
A program may use at most 128 MiB of HBM per device.

```python
import math
import jax
import jax.numpy as jnp
from jax import lax

BLOCK = 64
EX = 2
EY = 2
EZ = 4
SOURCES = 16
ITERS = 3
E_DEV = 16
FACE_DEV = 48
SPAN_X = 8
SPAN_Y = 16
ELEMENTS = 512
FACES = 1536


def draw_heat_source(key, part):
    device_count = FACES // FACE_DEV
    row_device = (jnp.arange(FACES) // FACE_DEV).astype(jnp.float32)
    device_ramp = (1.0 + 2.0 * row_device / max(device_count - 1, 1))[:, None]
    base_draw = jax.random.truncated_normal(key, -6.0, 6.0, (FACES, SOURCES * BLOCK), jnp.float32)
    return base_draw * device_ramp


def draw_stiffness(key, part):
    block_order = 6 * BLOCK
    identity = jnp.eye(block_order, dtype=jnp.float32)
    diag_high = 2.0
    scale_high = math.log(8.0)

    def draw_element(element_index):
        sub_key = jax.random.fold_in(key, element_index)
        key_off = jax.random.fold_in(sub_key, 1)
        key_diag = jax.random.fold_in(sub_key, 2)
        key_scale = jax.random.fold_in(sub_key, 3)
        weights = jax.random.uniform(key_off, (block_order, block_order), jnp.float32, -1.0, 3.0)
        weights = 0.5 * (weights + weights.T)
        diagonal = jax.random.uniform(key_diag, (block_order, 1), jnp.float32, 1.0, diag_high)
        element_scale = jnp.exp(jax.random.uniform(key_scale, (), jnp.float32, 0.0, scale_high))
        return element_scale * (identity * diagonal + (1.0 - identity) * (-0.3 / block_order) * weights)
    return lax.map(draw_element, jnp.arange(ELEMENTS))


def draw_element_faces(key, part):
    device_count = ELEMENTS // E_DEV
    inner = SPAN_Y // EY
    cell_keys = jax.random.split(jax.random.fold_in(key, 21), device_count)
    face_keys = jax.random.split(jax.random.fold_in(key, 22), device_count)
    cell_orders = jax.vmap(lambda sub_key: jax.random.permutation(sub_key, E_DEV))(cell_keys).astype(jnp.int32)
    face_orders = jax.vmap(lambda sub_key: jax.random.permutation(sub_key, 3 * E_DEV))(face_keys).astype(jnp.int32)
    element_ids = jnp.arange(ELEMENTS, dtype=jnp.int32)
    device_ids = element_ids // E_DEV
    cell = cell_orders[device_ids, element_ids % E_DEV]
    local_x = cell // (EY * EZ)
    local_y = cell // EZ % EY
    local_z = cell % EZ
    place_x = device_ids // inner * EX + local_x
    place_y = device_ids % inner * EY + local_y

    def face_of(spot_x, spot_y, spot_z, kind):
        spot_x = spot_x % SPAN_X
        spot_y = spot_y % SPAN_Y
        spot_z = spot_z % EZ
        owner = spot_x // EX * inner + spot_y // EY
        owner_cell = (spot_x % EX * EY + spot_y % EY) * EZ + spot_z
        return owner * FACE_DEV + face_orders[owner, owner_cell * 3 + kind]
    columns = [face_of(place_x, place_y, local_z, 0), face_of(place_x + 1, place_y, local_z, 0), face_of(place_x, place_y, local_z, 1), face_of(place_x, place_y + 1, local_z, 1), face_of(place_x, place_y, local_z, 2), face_of(place_x, place_y, local_z + 1, 2)]
    return jnp.stack(columns, axis=1).astype(jnp.int32)


def setup_inputs(seed: int = 0) -> dict:
    key_of = jax.random.split(jax.random.key(seed), 4)
    heat_source = draw_heat_source(jax.random.fold_in(key_of[3], 71), 0)
    stiffness = draw_stiffness(jax.random.fold_in(key_of[3], 71), 0)
    element_faces = draw_element_faces(jax.random.fold_in(key_of[3], 71), 0)
    return dict(heat_source=heat_source, stiffness=stiffness, element_faces=element_faces)


def operate(vector, stiffness, element_faces):
    face_count = vector.shape[0]
    flat_faces = element_faces.reshape(-1).astype(jnp.int32)
    blocks = vector[flat_faces].reshape(ELEMENTS, 6, SOURCES, BLOCK)
    matrix = stiffness.reshape(ELEMENTS, 6, BLOCK, 6, BLOCK)
    flux_terms = jnp.einsum("ekbjc,ejsc->eksb", matrix, blocks, precision=lax.Precision.HIGHEST, preferred_element_type=jnp.float32)
    return jax.ops.segment_sum(flux_terms.reshape(ELEMENTS * 6, SOURCES * BLOCK), flat_faces, num_segments=face_count)


def source_sum(first_vec, second_vec):
    return jnp.sum((first_vec * second_vec).reshape(-1, SOURCES, BLOCK), axis=(0, 2))


def spread(per_source):
    return jnp.repeat(per_source, BLOCK)[None, :]


def reference(heat_source, stiffness, element_faces):
    solution = jnp.zeros_like(heat_source)
    residual = heat_source
    direction = heat_source
    norm_now = source_sum(residual, residual)
    for iteration in range(ITERS):
        applied = operate(direction, stiffness, element_faces)
        step_size = norm_now / source_sum(direction, applied)
        solution = solution + spread(step_size) * direction
        residual = residual - spread(step_size) * applied
        norm_next = source_sum(residual, residual)
        direction = residual + spread(norm_next / norm_now) * direction
        norm_now = norm_next
    return solution, residual
```

```python
import jax
import jax.numpy as jnp
from jax import lax
from jax.experimental import pallas as pl
from jax.experimental.pallas import tpu as pltpu
from jax.sharding import PartitionSpec as P

BLOCK = 64
EX = 2
EY = 2
EZ = 4
HALF = BLOCK
LANES = 2 * BLOCK
F32 = jnp.float32
BF16 = jnp.bfloat16
MESH = pl.DeviceIdType.MESH
AHEAD = 2
MIDDLE = 9


def index_tables(faces, base, count, face_dev, nx, ny, idx):
    sub = lax.broadcasted_iota(jnp.int32, (count, count), 0)
    lane = lax.broadcasted_iota(jnp.int32, (count, count), 1)
    eye = sub == lane
    slots = 6 * count
    rows = [faces[k : k + 1, :] for k in range(6)]
    cols = [jnp.sum(jnp.where(eye, r, 0), axis=1, keepdims=True) for r in rows]
    idx[...] = jnp.zeros(idx.shape, jnp.int32)
    starts = [0, nx, 2 * nx, 2 * nx + ny]
    wide = lax.broadcasted_iota(jnp.int32, (count, LANES), 1)
    wide_sub = lax.broadcasted_iota(jnp.int32, (count, LANES), 0)
    for k, other, role in ((4, 5, 1), (5, 4, 0)):
        match = (cols[other] == rows[k]).astype(jnp.int32)
        place = jnp.sum(match * sub, axis=0, keepdims=True)
        idx[1 - role : 2 - role, 0:count] = role * count + place
        idx[7 - role : 8 - role, 0:count] = rows[k] - base
    owned = (cols[4] - base) == wide
    inverse = jnp.sum(jnp.where(owned, wide_sub, 0), axis=0, keepdims=True)
    for axis in range(2):
        low, up = 2 * axis, 2 * axis + 1
        near, far = 2 + axis, 4 + axis
        match_low = (cols[up] == rows[low]).astype(jnp.int32)
        match_up = (cols[low] == rows[up]).astype(jnp.int32)
        has = jnp.sum(match_low, axis=0, keepdims=True) > 0
        has_c = jnp.sum(match_up, axis=1, keepdims=True) > 0
        partner = jnp.sum((match_low + match_up) * sub, axis=0, keepdims=True)
        idx[near : near + 1, 0:count] = near * count + partner
        idx[6 + near : 7 + near, 0:count] = jnp.where(has, rows[low], rows[up]) - base
        idx[19 + axis : 20 + axis, 0:count] = jnp.where(has, low, up)
        spot = []
        for k, away, away_c in ((low, ~has, ~has_c), (up, has, has_c)):
            before = jnp.where(away_c & (cols[k] < rows[k]), 1, 0)
            rank = jnp.sum(before, axis=0, keepdims=True)
            before_c = jnp.where(away & (rows[k] < cols[k]), 1, 0)
            rank_c = jnp.sum(before_c, axis=1, keepdims=True)
            chosen = away_c & (rank_c == lane)
            listed = jnp.sum(jnp.where(chosen, far * count + sub, 0), axis=0, keepdims=True)
            idx[12 + k : 13 + k, 0:count] = listed
            spot.append(rank)
            if k == low:
                traces = jnp.where(chosen, cols[k] - base, 0)
                idx[17 + axis : 18 + axis, 0:count] = jnp.sum(traces, axis=0, keepdims=True)
        first = face_dev + (0 if axis == 0 else nx)
        idx[far : far + 1, 0:count] = slots + jnp.where(has, starts[up] + spot[1], starts[low] + spot[0])
        idx[6 + far : 7 + far, 0:count] = jnp.where(has, first + spot[1], rows[low] - base)
        owned = (cols[low] - base) == wide
        slot_c = jnp.where(has_c, near, far) * count + wide_sub
        inverse = inverse + jnp.sum(jnp.where(owned, slot_c, 0), axis=0, keepdims=True)
    idx[16:17, :] = inverse
    idx[0:4, :] = jnp.clip(idx[0:4, :], 0, slots - 1)
    idx[4:6, :] = jnp.clip(idx[4:6, :], slots, slots + 2 * (nx + ny) - 1)
    idx[6:12, :] = jnp.clip(idx[6:12, :], 0, face_dev + nx + ny - 1)
    idx[12:17, :] = jnp.clip(idx[12:17, :], 0, slots - 1)
    idx[17:19, :] = jnp.clip(idx[17:19, :], 0, face_dev - 1)
    idx[19:20, :] = jnp.clip(idx[19:20, :], 0, 1)
    idx[20:21, :] = jnp.clip(idx[20:21, :], 2, 3)


def make_kernel(outer, inner, count, face_dev, groups, nx, ny):
    slots = 6 * count
    parts = outer * inner

    def kernel(heat_hbm, faces_hbm, stiff_ref,
               fin0, fin1, fin2, fin3, coef0, coef1, coef2, coef3, coef4, coef5, coef6,
               heat_ref, faces_ref, raw, high, low, diag, table, v0, v1, v2, flux, flux2, flux3, partial,
               idx_v, idx, send0, recv0, sends, recv1, recv2, recv3, sum_tx, sum_rx,
               fin,
               in_sem, out_sem, raw_sem, idx_sem, s0_sem, r0_sem, ss_sem, rr_sem,
               sum_ss, sum_rs):
        gx = lax.axis_index("gx")
        gy = lax.axis_index("gy")
        x_next = (lax.rem(gx + 1, outer), gy)
        x_prev = (lax.rem(gx + outer - 1, outer), gy)
        y_next = (gx, lax.rem(gy + 1, inner))
        y_prev = (gx, lax.rem(gy + inner - 1, inner))
        recvs = (recv1, recv2, recv3)

        get_heat = pltpu.make_async_copy(heat_hbm, heat_ref, in_sem.at[0])
        get_faces = pltpu.make_async_copy(faces_hbm, faces_ref, in_sem.at[1])
        get_faces.start()
        get_heat.start()

        def other(d):
            return (lax.rem(gx + d // inner, outer), lax.rem(gy + d % inner, inner))

        def raw_copy(e):
            return pltpu.make_async_copy(stiff_ref.at[e], raw.at[e], raw_sem.at[e])

        for e in range(count):
            raw_copy(e).start()
        barrier = pltpu.get_barrier_semaphore()
        for d in range(1, parts):
            pl.semaphore_signal(barrier, inc=1, device_id=other(d), device_id_type=MESH)

        base = (gx * inner + gy) * face_dev
        get_faces.wait()
        index_tables(faces_ref[...], base, count, face_dev, nx, ny, idx_v)
        to_smem = pltpu.make_async_copy(idx_v, idx, idx_sem)
        to_smem.start()

        def rows_of(f):
            return pl.ds((f // 8) * groups * 8 + f % 8, groups, stride=8)

        lane = lax.broadcasted_iota(jnp.int32, (8, LANES), 1)
        sub = lax.broadcasted_iota(jnp.int32, (8, LANES), 0)
        left = lane < HALF
        shifted = lane - sub
        on_diag = lane % 8 == sub

        def swap(a):
            return pltpu.roll(a, HALF, 1)

        def split(e):
            raw_copy(e).wait()
            for c in range(3):
                acc = None
                for k in range(6):
                    a = raw[e, k * HALF : (k + 1) * HALF, c * LANES : (c + 1) * LANES]
                    if k // 2 == c:
                        pieces = []
                        for i in range(HALF // 8):
                            piece = a[8 * i : 8 * i + 8]
                            mask = shifted == (k % 2) * HALF + 8 * i
                            acc = piece if acc is None else jnp.where(mask, piece, acc)
                            pieces.append(jnp.where(mask, 0.0, piece))
                        a = jnp.concatenate(pieces, axis=0)
                    h = a.astype(BF16)
                    high[e, c, k] = h
                    low[e, c, k] = (a - h.astype(F32)).astype(BF16)
                d = jnp.broadcast_to(
                    jnp.sum(jnp.where(on_diag, acc, 0.0), axis=0, keepdims=True), (8, LANES)
                )
                turned = swap(d)
                diag[e, 2 * c] = jnp.where(left, d, turned)
                diag[e, 2 * c + 1] = jnp.where(left, turned, d)

        def split_only(e, carry):
            split(e)
            return carry

        lax.fori_loop(0, AHEAD, split_only, 0, unroll=True)

        get_heat.wait()
        gamma0 = jnp.zeros((8, LANES), F32)
        for f in range(face_dev):
            t = heat_ref[rows_of(f), :]
            table[f] = t
            gamma0 = gamma0 + t * t
        to_smem.wait()

        def remote(src, dst, ssem, rsem, device):
            return pltpu.make_async_remote_copy(
                src_ref=src, dst_ref=dst, send_sem=ssem, recv_sem=rsem,
                device_id=device, device_id_type=MESH,
            )

        first = [
            remote(send0.at[pl.ds(0, nx)], recv0.at[pl.ds(0, nx)], s0_sem.at[0], r0_sem.at[0], x_prev),
            remote(send0.at[pl.ds(nx, ny)], recv0.at[pl.ds(nx, ny)], s0_sem.at[1], r0_sem.at[1], y_prev),
        ]
        def halves_of(tiles):
            evens, odds = [], []
            for a, b in zip(tiles[0::2], tiles[1::2]):
                evens.append(jnp.where(left, a, swap(b)))
                odds.append(jnp.where(left, swap(a), b))
            if len(evens) > 1:
                evens, odds = [jnp.concatenate(evens, axis=1)], [jnp.concatenate(odds, axis=1)]
            x = jnp.concatenate([evens[0], odds[0]], axis=0)
            xh = x.astype(BF16)
            return xh, (x - xh.astype(F32)).astype(BF16)

        def weights(ref, e, ks):
            return jnp.concatenate(
                [jnp.concatenate([ref[e, c, k] for k in ks], axis=0) for c in range(3)], axis=1
            )

        def near_product(tiles, e):
            xh, xl = halves_of(tiles)
            ks = (4, 5, idx[19, e], idx[20, e])
            both = jnp.concatenate([xh, xl], axis=0)
            p = jnp.dot(both, weights(high, e, ks), preferred_element_type=F32)
            q = jnp.dot(xh, weights(low, e, ks), preferred_element_type=F32)
            partial[e] = p[0:16] + (p[16:32] + q)

        def far_product(new, tiles, full, e, dot):
            xh, xl = halves_of(tiles)
            kx, ky = idx[19, e], idx[20, e]
            ks = (1 - kx, 5 - ky)
            both = jnp.concatenate(
                [jnp.concatenate([xh, xh], axis=1),
                 jnp.concatenate([xl, jnp.zeros_like(xl)], axis=1)], axis=0
            )
            w = jnp.concatenate([weights(high, e, ks), weights(low, e, ks)], axis=0)
            p = jnp.dot(both, w, preferred_element_type=F32)
            y = partial[e] + (p[0:16] + p[16:32])
            out = []
            for axis in range(3):
                part = y[:, axis * LANES : (axis + 1) * LANES]
                ev, od = part[0:8], part[8:16]
                out.append(jnp.where(left, ev, swap(od)))
                out.append(jnp.where(left, swap(ev), od))
            by_role = [
                out[4], out[5],
                jnp.where(kx == 0, out[0], out[1]), jnp.where(ky == 2, out[2], out[3]),
                jnp.where(kx == 0, out[1], out[0]), jnp.where(ky == 2, out[3], out[2]),
            ]
            kinds = (4, 5, kx, ky, *ks)
            for role in range(6):
                f = by_role[role] + full[role] * diag[e, kinds[role]]
                new[role * count + e] = f
                if dot is not None:
                    dot = dot + f * full[role]
            return dot

        spots = [0, nx, 2 * nx, 2 * nx + ny]
        plan = [(0, nx, x_prev, 1), (1, nx, x_next, 0), (2, ny, y_prev, 3), (3, ny, y_next, 2)]

        def exchange(phase, flux, kinds):
            copies = []
            for kind, rows, target, lands in plan:
                if kind not in kinds:
                    continue
                for r in range(rows):
                    sends[phase, spots[kind] + r] = flux[idx[12 + kind, r]]
                copies.append(
                    remote(
                        sends.at[phase, pl.ds(spots[kind], rows)],
                        recvs[phase].at[pl.ds(spots[lands], rows)],
                        ss_sem.at[phase, kind], rr_sem.at[phase, lands], target,
                    )
                )
                copies[-1].start()
            return copies

        def halves(tile):
            even = jnp.sum(jnp.where(left, tile, 0.0), axis=1, keepdims=True)
            odd = jnp.sum(jnp.where(left, 0.0, tile), axis=1, keepdims=True)
            return even, odd

        spot = lane % 16
        mine = lane // 16 == sub

        def packed(tiles):
            out = jnp.zeros((8, LANES), F32)
            for m, t in enumerate(tiles):
                even, odd = halves(t)
                out = jnp.where(spot == 2 * m, even, out)
                out = jnp.where(spot == 2 * m + 1, odd, out)
            return out

        def unpacked(row, m):
            own = jnp.where(mine, jnp.broadcast_to(row, (8, LANES)), 0.0)
            even = jnp.sum(jnp.where(spot == 2 * m, own, 0.0), axis=1, keepdims=True)
            odd = jnp.sum(jnp.where(spot == 2 * m + 1, own, 0.0), axis=1, keepdims=True)
            return jnp.where(left, even, odd)

        def sum_start(turn, value):
            sum_tx[turn] = jnp.sum(jnp.where(mine, value, 0.0), axis=0, keepdims=True)
            copies = []
            for d in range(1, parts):
                copies.append(remote(sum_tx.at[turn], sum_rx.at[turn, d - 1], sum_ss.at[turn, d - 1],
                                     sum_rs.at[turn, d - 1], other(d)))
                copies[-1].start()
            return copies

        def sum_end(turn, copies):
            for c in copies:
                c.wait_recv()
            return sum_tx[turn] + jnp.sum(sum_rx[turn], axis=0)

        zero = jnp.zeros((8, LANES), F32)
        every = (0, 1, 2, 3)

        def near_zero(e):
            tiles = []
            for role in range(4):
                t = table[idx[6 + role, e]]
                v0[role * count + e] = t
                tiles.append(t)
            near_product(tiles, e)

        def far_zero(e, dot):
            full = [v0[role * count + e] for role in range(4)]
            for role in (4, 5):
                t = table[idx[6 + role, e]]
                v0[role * count + e] = t
                full.append(t)
            return far_product(flux, full[4:], full, e, dot)

        lag = AHEAD - 1

        def near_step(e, carry):
            split(e)
            near_zero(e - lag)
            return carry

        def near_last(e, carry):
            near_zero(e)
            return carry

        near_zero(0)
        lax.fori_loop(AHEAD, MIDDLE, near_step, 0, unroll=True)
        for r in range(nx):
            send0[r] = table[idx[17, r]]
        for r in range(ny):
            send0[nx + r] = table[idx[18, r]]
        pl.semaphore_wait(barrier, parts - 1)
        for c in first:
            c.start()
        lax.fori_loop(MIDDLE, count, near_step, 0, unroll=True)
        lax.fori_loop(count - lag, count, near_last, 0, unroll=True)
        for c in first:
            c.wait_recv()
        for r in range(nx + ny):
            table[face_dev + r] = recv0[r]
        delta0 = lax.fori_loop(0, count, far_zero, zero, unroll=True)
        swap1 = exchange(0, flux, every)
        sum1 = sum_start(0, packed([gamma0, delta0]))

        def apply(v, old, recv, new, copies):
            def near(e, carry):
                tiles = []
                for role in range(4):
                    at = role * count + e
                    t = old[at] + old[idx[role, e]]
                    v[at] = t
                    tiles.append(t)
                near_product(tiles, e)
                return carry

            def far(e, carry):
                full = [v[role * count + e] for role in range(4)]
                for role in (4, 5):
                    at = role * count + e
                    t = old[at] + recv[idx[role, e] - slots]
                    v[at] = t
                    full.append(t)
                far_product(new, full[4:], full, e, None)
                return carry

            lax.fori_loop(0, count, near, 0, unroll=True)
            for c in copies:
                c.wait_recv()
            lax.fori_loop(0, count, far, 0, unroll=True)

        apply(v1, flux, recv1, flux2, swap1)
        swap2 = exchange(1, flux2, every)
        apply(v2, flux2, recv2, flux3, swap2)
        swap3 = exchange(2, flux3, (1, 3))
        total = sum_end(0, sum1)
        gamma0 = unpacked(total, 0)
        delta0 = unpacked(total, 1)
        alpha0 = gamma0 / delta0
        inverse0 = delta0 / gamma0

        def inner_products(e, carry):
            dot, once, twice = carry
            for role in range(6):
                at = role * count + e
                one = v1[at]
                w = one - alpha0 * v2[at]
                dot = dot + (flux2[at] - alpha0 * flux3[at]) * w
                if role == 1:
                    continue
                r1 = v0[at] - alpha0 * one
                terms = (r1 * r1, r1 * w, w * w)
                if role == 0:
                    once = tuple(a + t for a, t in zip(once, terms))
                else:
                    twice = tuple(a + t for a, t in zip(twice, terms))
            return dot, once, twice

        dot_e, once, twice = lax.fori_loop(
            0, count, inner_products, (zero, (zero,) * 3, (zero,) * 3), unroll=4
        )
        dots = [a + 0.5 * b for a, b in zip(once, twice)]
        sum2 = sum_start(1, packed([*dots, dot_e]))
        for c in swap3:
            c.wait_recv()
        for kind, rows, _, _ in plan:
            if kind in (0, 2):
                for r in range(rows):
                    flux3[slots + spots[kind] + r] = recv3[spots[kind] + r]

        def gather(fc, carry):
            at = idx[16, fc]
            pair = idx[lax.div(at, count), lax.rem(at, count)]
            x0, one, two = v0[at], v1[at], v2[at]
            rows = rows_of(fc)
            fin[0, rows, :] = x0
            fin[1, rows, :] = x0 - alpha0 * one
            fin[2, rows, :] = one - alpha0 * two
            fin[3, rows, :] = two - alpha0 * (flux3[at] + flux3[pair])
            return carry

        lax.fori_loop(0, face_dev, gather, 0, unroll=4)
        puts = [
            pltpu.make_async_copy(fin.at[m], to, out_sem.at[m])
            for m, to in enumerate((fin0, fin1, fin2, fin3))
        ]
        for c in puts:
            c.start()
        for c in [*first, *swap1, *swap2, *swap3, *sum1, *sum2]:
            c.wait_send()
        for c in puts:
            c.wait()

        total = sum_end(1, sum2)
        g1, d1, ww, ee = [unpacked(total, m) for m in range(4)]
        rv = -g1 * inverse0
        wv = (rv - d1) * inverse0
        vv = (delta0 - rv) * inverse0
        f = (wv - ww) * inverse0
        g = (vv - wv) * inverse0
        b0 = g1 / gamma0
        pap = d1 + 2.0 * b0 * rv + b0 * b0 * delta0
        a1 = g1 / pap
        rs = d1 + b0 * rv
        s2 = ww + b0 * (2.0 * wv + b0 * vv)
        g2 = g1 - 2.0 * a1 * rs + a1 * a1 * s2
        b1 = g2 / g1
        rar = d1 - 2.0 * a1 * (ww + b0 * wv) + a1 * a1 * (ee + b0 * (2.0 * f + b0 * g))
        pap2 = rar + 2.0 * b1 * (rs - a1 * s2) + b1 * b1 * pap
        a2 = g2 / pap2
        back = a1 * b0 * inverse0
        turn = b1 * b0 - back
        mixed = 1.0 + back + b1
        shift = a2 * turn * inverse0
        scales = (
            alpha0 + a1 * b0 + a2 * turn, a1 + a2 * mixed, -a2 * a1,
            -back - shift, 1.0 + back + shift, -a1 - a2 * mixed, a2 * a1,
        )
        for to, value in zip((coef0, coef1, coef2, coef3, coef4, coef5, coef6), scales):
            to[...] = value

    return kernel


def local(heat_source, stiffness, element_faces):
    face_dev, width = heat_source.shape
    count, order = stiffness.shape[0], stiffness.shape[1]
    groups = width // LANES
    outer = lax.axis_size("gx")
    inner = lax.axis_size("gy")
    nx, ny = EY * EZ, EX * EZ
    slots = 6 * count
    ext = 2 * (nx + ny)
    tile = (groups, LANES)
    flat = (face_dev * groups, LANES)
    vmem = lambda *s: pltpu.VMEM(s, F32)
    dma = lambda *s: pltpu.SemaphoreType.DMA(s)
    tiled = heat_source.reshape(face_dev // 8, 8, groups, LANES).transpose(0, 2, 1, 3)
    outs = pl.pallas_call(
        make_kernel(outer, inner, count, face_dev, groups, nx, ny),
        name="cg",
        out_shape=(
            *(jax.ShapeDtypeStruct(flat, F32),) * 4,
            *(jax.ShapeDtypeStruct(tile, F32),) * 7,
        ),
        in_specs=[
            pl.BlockSpec(memory_space=pltpu.HBM),
            pl.BlockSpec(memory_space=pltpu.HBM),
            pl.BlockSpec(memory_space=pltpu.HBM),
        ],
        out_specs=(
            *(pl.BlockSpec(memory_space=pltpu.HBM),) * 4,
            *(pl.BlockSpec(memory_space=pltpu.VMEM),) * 7,
        ),
        scratch_shapes=[
            vmem(*flat),
            pltpu.VMEM((6, count), jnp.int32),
            vmem(count, order, order),
            pltpu.VMEM((count, 3, 6, HALF, LANES), BF16),
            pltpu.VMEM((count, 3, 6, HALF, LANES), BF16),
            vmem(count, 6, 8, LANES),
            vmem(face_dev + nx + ny, *tile),
            vmem(slots, *tile),
            vmem(slots, *tile),
            vmem(slots, *tile),
            vmem(slots, *tile),
            vmem(slots, *tile),
            vmem(slots + ext, *tile),
            vmem(count, 16, order),
            pltpu.VMEM((24, LANES), jnp.int32),
            pltpu.SMEM((24, LANES), jnp.int32),
            vmem(nx + ny, *tile),
            vmem(nx + ny, *tile),
            vmem(3, ext, *tile),
            vmem(ext, *tile),
            vmem(ext, *tile),
            vmem(ext, *tile),
            vmem(2, 1, LANES),
            vmem(2, outer * inner - 1, 1, LANES),
            vmem(4, *flat),
            dma(2), dma(4),
            dma(count), pltpu.SemaphoreType.DMA,
            dma(2), dma(2), dma(3, 4), dma(3, 4),
            dma(2, outer * inner - 1), dma(2, outer * inner - 1),
        ],
        compiler_params=pltpu.CompilerParams(
            collective_id=0, has_side_effects=True, vmem_limit_bytes=67043328
        ),
    )(tiled.reshape(flat), element_faces.T, stiffness)

    x0, r1, w, last = [a.reshape(face_dev // 8, groups, 8, LANES) for a in outs[:4]]
    c = [a.reshape(1, groups, 1, LANES) for a in outs[4:]]

    def untile(a):
        return a.transpose(0, 2, 1, 3).reshape(face_dev, width)

    sol = c[0] * x0 + c[1] * r1 + c[2] * w
    res = c[3] * x0 + c[4] * r1 + c[5] * w + c[6] * last
    return untile(sol), untile(res)


def solution(mesh):
    return jax.shard_map(
        local,
        mesh=mesh,
        in_specs=(P(("gx", "gy"), None), P(("gx", "gy"), None, None), P(("gx", "gy"), None)),
        out_specs=(P(("gx", "gy"), None), P(("gx", "gy"), None)),
        check_vma=False,
    )
```
